256 devices in a mesh: row: 16 (over z_hi, x), col: 16 (over z_lo, y, core).
Axes of the slice: x: 4, y: 4, z: 8 (z_hi: 4, z_lo: 2; z = z_hi * 2 + z_lo), core: 2. Of those that a mesh axis runs over, the one named last changes fastest.
Arguments:
- visible_data: bfloat16 [512, 32768], P('col', 'row'), may hold values from 0 to 1
- hidden_uniform: float32 [512, 16384], P('row', 'col'), may hold values from 0.01 to 0.99
- visible_uniform: float32 [512, 32768], P('col', 'row'), may hold values from 0.01 to 0.99
- weights: bfloat16 [32768, 16384], P('row', 'col'), may hold values from -0.03125 to 0.03125
- visible_bias: float32 [32768], P('row'), may hold values from -4 to 4
- hidden_bias: float32 [16384], P('col'), may hold values from -4 to 4
Outputs:
- grad_weights: bfloat16 [32768, 16384], P('row', 'col')
- grad_visible: float32 [32768], P('row')
- grad_hidden: float32 [16384], P('col')
- hidden_sample: bfloat16 [512, 16384], P('row', 'col')
- reconstruction: bfloat16 [512, 32768], P('col', 'row')
The draws below stay inside these ranges and needn't reach their ends.
All inputs are finite; a program needn't handle non-finite values.
Results may differ from the reference program's by a relative error of at most 0.0034.
Values may be sent and summed in bfloat16 or wider, within the bound.
No kernel may reach another device: no remote copies, remote signals or barrier semaphores. Data moves between devices by JAX's collectives and lax.ppermute only.
A program may use at most 64 MiB of HBM per device.

```python
import jax
import jax.numpy as jnp

V = 32768
H = 16384
BATCH = 512


def block_scale(key, dims, shards, low, largest):
    gain, own = 1.0, jax.random.fold_in(key, 6)
    for dim, blocks in shards:
        draws = jnp.exp(jax.random.uniform(jax.random.fold_in(own, dim), (blocks,), jnp.float32, low / len(shards), largest / len(shards)))
        gain = gain * jnp.repeat(draws, dims[dim] // blocks).reshape([-1 if axis == dim else 1 for axis in range(len(dims))])
    return gain


def noise(rng, extent, spread, bound, cuts=(), dtype=jnp.bfloat16):
    values = jax.random.normal(rng, extent, jnp.float32) * spread
    if len(cuts) > 0:
        values = block_scale(rng, extent, cuts, -0.22, 0.18) * values
    return jnp.clip(values, min=-bound, max=bound).astype(dtype)


def setup_inputs(seed: int = 0) -> dict:
    splits = jax.random.split(jax.random.key(seed), 7)
    visible_data = jnp.clip(1.0 * jax.random.uniform(splits[0], (BATCH, V), jnp.float32) ** block_scale(splits[0], (BATCH, V), ((0, 16), (1, 16)), -0.2, 0.2), 0.0, 1.0).astype(jnp.bfloat16)
    hidden_uniform = jnp.clip(0.01 + 0.98 * jax.random.uniform(splits[1], (BATCH, H), jnp.float32) ** block_scale(splits[1], (BATCH, H), ((0, 16), (1, 16)), -0.2, 0.2), 0.01, 0.99)
    visible_uniform = jnp.clip(0.01 + 0.98 * jax.random.uniform(splits[2], (BATCH, V), jnp.float32) ** block_scale(splits[2], (BATCH, V), ((0, 16), (1, 16)), -0.2, 0.2), 0.01, 0.99)
    weights = noise(splits[3], (V, H), V ** -0.5, 0.03125, ((0, 16), (1, 16)))
    visible_bias = noise(splits[4], (V,), 1.0, 4.0, ((0, 16),), jnp.float32)
    hidden_bias = noise(splits[5], (H,), 1.0, 4.0, ((0, 16),), jnp.float32)
    return {"visible_data": visible_data, "hidden_uniform": hidden_uniform, "visible_uniform": visible_uniform, "weights": weights, "visible_bias": visible_bias, "hidden_bias": hidden_bias}


def relaxed(field, uniform):
    return jax.nn.sigmoid(2.0 * (field + jnp.log(uniform) - jnp.log1p(-uniform)))


def reference(visible_data, hidden_uniform, visible_uniform, weights, visible_bias, hidden_bias):
    field_pos = jnp.dot(visible_data, weights, preferred_element_type=jnp.float32) + hidden_bias
    probs_pos = jax.nn.sigmoid(field_pos).astype(jnp.bfloat16)
    hidden_sample = relaxed(field_pos, hidden_uniform).astype(jnp.bfloat16)
    field_neg = jnp.dot(hidden_sample, weights.T, preferred_element_type=jnp.float32) + visible_bias
    reconstruction = relaxed(field_neg, visible_uniform).astype(jnp.bfloat16)
    field_back = jnp.dot(reconstruction, weights, preferred_element_type=jnp.float32) + hidden_bias
    probs_neg = jax.nn.sigmoid(field_back).astype(jnp.bfloat16)
    positive = jnp.dot(visible_data.T, probs_pos, preferred_element_type=jnp.float32)
    negative = jnp.dot(reconstruction.T, probs_neg, preferred_element_type=jnp.float32)
    grad_weights = ((positive - negative) / BATCH).astype(jnp.bfloat16)
    grad_visible = jnp.mean(visible_data.astype(jnp.float32) - reconstruction.astype(jnp.float32), axis=0)
    grad_hidden = jnp.mean(probs_pos.astype(jnp.float32) - probs_neg.astype(jnp.float32), axis=0)
    return grad_weights, grad_visible, grad_hidden, hidden_sample, reconstruction
```

```python
import functools

import jax
import jax.numpy as jnp
from jax import lax
from jax.experimental import pallas as pl
from jax.experimental.pallas import tpu as pltpu
from jax.sharding import PartitionSpec as P

F32, BF16 = jnp.float32, jnp.bfloat16


def flip(array, axis, bits):
    return lax.ppermute(array, axis, [(i, i ^ bits) for i in range(16)])


def spread(array, axis, step):
    return [array] + [flip(array, axis, s * step) for s in (1, 2, 3)]


def row_to_index(p):
    return (p & 3) * 4 + (p >> 2)


def col_to_index(p):
    return ((p >> 1) & 3) * 4 + (p >> 3) * 2 + (p & 1)


def put_rows(q, acc, outs, rows, to_row):
    for piece in range(4):
        for sub in range(4):
            if to_row:
                source = col_to_index((sub * 4 + piece) ^ q)
            else:
                source = row_to_index(((sub >> 1) * 8 + piece * 2 + (sub & 1)) ^ q)
            block = acc[pl.ds(pl.multiple_of(source * rows, rows), rows), :]
            out = outs[piece]
            out[sub * rows : (sub + 1) * rows, :] = block.astype(out.dtype)


def forward_kernel(steps, rows, q_ref, a0, a1, a2, a3, own, other, *rest):
    outs, (lhs, acc) = rest[:4], rest[4:]
    step = pl.program_id(0)
    n = a0.shape[0]

    @pl.when(step == 0)
    def _():
        for i, a in enumerate((a0, a1, a2, a3)):
            lhs[i * n : (i + 1) * n, :] = a[...]

    @pl.when(step < steps)
    def _():
        acc[...] = jnp.dot(lhs[...], own[...], preferred_element_type=F32)

    @pl.when(step >= steps)
    def _():
        acc[...] = jnp.dot(lhs[...], other[...], preferred_element_type=F32)

    put_rows(q_ref[0], acc, outs, rows, True)


def forward(q, pieces, own, other, tile=512):
    n, depth = pieces[0].shape
    width = own.shape[1]
    steps = width // tile
    whole = pl.BlockSpec((n, depth), lambda j, q: (0, 0))
    out = [jax.ShapeDtypeStruct((n, 2 * width), F32)] + [
        jax.ShapeDtypeStruct((n, 2 * width), BF16) for _ in range(3)
    ]
    return pl.pallas_call(
        functools.partial(forward_kernel, steps, n // 4),
        out_shape=out,
        grid_spec=pltpu.PrefetchScalarGridSpec(
            num_scalar_prefetch=1,
            grid=(2 * steps,),
            in_specs=[whole] * 4
            + [
                pl.BlockSpec((depth, tile), lambda j, q: (0, jnp.minimum(j, steps - 1))),
                pl.BlockSpec((depth, tile), lambda j, q: (0, jnp.maximum(j - steps, 0))),
            ],
            out_specs=[pl.BlockSpec((n, tile), lambda j, q: (0, j))] * 4,
            scratch_shapes=[pltpu.VMEM((4 * n, depth), BF16), pltpu.VMEM((4 * n, tile), F32)],
        ),
        compiler_params=pltpu.CompilerParams(vmem_limit_bytes=40 << 20),
        cost_estimate=pl.CostEstimate(
            flops=2 * 4 * n * depth * 2 * width,
            bytes_accessed=4 * depth * width + 10 * n * depth + 10 * n * width,
            transcendentals=0,
        ),
    )(q, *pieces, own, other)


def backward_kernel(rows, q_ref, a0, a1, a2, a3, own, other, *rest):
    outs, (lhs, acc) = rest[:4], rest[4:]
    n = a0.shape[0]

    @pl.when(pl.program_id(0) == 0)
    def _():
        for i, a in enumerate((a0, a1, a2, a3)):
            lhs[i * n : (i + 1) * n, :] = a[...]

    width = own.shape[1]
    transposed = (((1,), (1,)), ((), ()))
    acc[...] = lax.dot_general(
        lhs[:, :width], own[...], transposed, preferred_element_type=F32
    ) + lax.dot_general(lhs[:, width:], other[...], transposed, preferred_element_type=F32)
    put_rows(q_ref[0], acc, outs, rows, False)


def backward(q, pieces, own, other, tile=512):
    n, depth = pieces[0].shape
    height, width = own.shape
    whole = pl.BlockSpec((n, depth), lambda j, q: (0, 0))
    out = [jax.ShapeDtypeStruct((n, height), F32)] + [
        jax.ShapeDtypeStruct((n, height), BF16) for _ in range(3)
    ]
    return pl.pallas_call(
        functools.partial(backward_kernel, n // 4),
        out_shape=out,
        grid_spec=pltpu.PrefetchScalarGridSpec(
            num_scalar_prefetch=1,
            grid=(height // tile,),
            in_specs=[whole] * 4 + [pl.BlockSpec((tile, width), lambda j, q: (j, 0))] * 2,
            out_specs=[pl.BlockSpec((n, tile), lambda j, q: (0, j))] * 4,
            scratch_shapes=[pltpu.VMEM((4 * n, depth), BF16), pltpu.VMEM((4 * n, tile), F32)],
        ),
        compiler_params=pltpu.CompilerParams(vmem_limit_bytes=40 << 20),
        cost_estimate=pl.CostEstimate(
            flops=2 * 4 * n * depth * height,
            bytes_accessed=4 * height * width + 10 * n * depth + 10 * n * height,
            transcendentals=0,
        ),
    )(q, *pieces, own, other)


def gradient_kernel(total, rows, q_ref, *refs):
    (v, v_other, r, r_other, pos, neg) = (refs[0:4], refs[4:8], refs[8:12], refs[12:16], refs[16:20], refs[20:24])
    grad, grad_visible, grad_hidden, raw, probs, left = refs[24:]
    n = v[0].shape[0]
    half = 4 * n
    q = q_ref[0]

    @pl.when(pl.program_id(0) == 0)
    def _():
        for sign, pieces in enumerate((pos, neg)):
            for i, piece in enumerate(pieces):
                raw[i * 2 * n : (i + 1) * 2 * n, :] = piece[...]
            for other in range(2):
                for p in range(16):
                    source = row_to_index(p ^ q ^ other) * 2 + other
                    at = (sign * 2 + other) * half + col_to_index(p) * rows
                    block = raw[pl.ds(pl.multiple_of(source * rows, rows), rows), :]
                    probs[at : at + rows, :] = -block if sign else block
        grad_hidden[...] = jnp.sum(probs[...].astype(F32), axis=0, keepdims=True) / total

    for k, pieces in enumerate((v, v_other, r, r_other)):
        for i, piece in enumerate(pieces):
            left[k * half + i * n : k * half + (i + 1) * n, :] = piece[...]
    values = left[...]
    grad[...] = (
        lax.dot_general(values, probs[...], (((0,), (0,)), ((), ())), preferred_element_type=F32)
        / total
    ).astype(grad.dtype)
    grad_visible[...] = (
        jnp.sum(left[: 2 * half, :].astype(F32), axis=0, keepdims=True)
        - jnp.sum(left[2 * half :, :].astype(F32), axis=0, keepdims=True)
    ) / total


def gradient(q, total, v, v_other, r, r_other, pos, neg, tile=256):
    n, height = v[0].shape
    width = pos[0].shape[1]
    return pl.pallas_call(
        functools.partial(gradient_kernel, total, n // 4),
        out_shape=[
            jax.ShapeDtypeStruct((height, width), BF16),
            jax.ShapeDtypeStruct((1, height), F32),
            jax.ShapeDtypeStruct((1, width), F32),
        ],
        grid_spec=pltpu.PrefetchScalarGridSpec(
            num_scalar_prefetch=1,
            grid=(height // tile,),
            in_specs=[pl.BlockSpec((n, tile), lambda j, q: (0, j))] * 16
            + [pl.BlockSpec((2 * n, width), lambda j, q: (0, 0))] * 8,
            out_specs=[
                pl.BlockSpec((tile, width), lambda j, q: (j, 0)),
                pl.BlockSpec((1, tile), lambda j, q: (0, j)),
                pl.BlockSpec((1, width), lambda j, q: (0, 0)),
            ],
            scratch_shapes=[
                pltpu.VMEM((8 * n, width), BF16),
                pltpu.VMEM((16 * n, width), BF16),
                pltpu.VMEM((16 * n, tile), BF16),
            ],
        ),
        compiler_params=pltpu.CompilerParams(vmem_limit_bytes=40 << 20),
        cost_estimate=pl.CostEstimate(
            flops=2 * 16 * n * height * width,
            bytes_accessed=2 * height * width + 32 * n * height + 32 * n * width,
            transcendentals=0,
        ),
    )(q, *v, *v_other, *r, *r_other, *pos, *neg)


def on_device(visible_data, hidden_uniform, visible_uniform, weights, visible_bias, hidden_bias):
    row, col = lax.axis_index("row"), lax.axis_index("col")
    core = col & 1
    block, visibles = visible_data.shape
    hiddens = weights.shape[1]
    half = block // 2
    total = block * 16
    q = (row ^ col).astype(jnp.int32).reshape(1)

    def cut(array):
        return (
            lax.dynamic_slice_in_dim(array, core * half, half, 0),
            lax.dynamic_slice_in_dim(array, (1 - core) * half, half, 0),
        )

    def swap(array):
        return flip(array, "col", 1)

    def whole_block(mine, others):
        first = jnp.where(core == 0, mine, others)
        return jnp.concatenate([first, jnp.where(core == 0, others, mine)], axis=0)

    mine, others = cut(visible_data)
    visible = jnp.concatenate([mine, swap(others)], axis=0)
    weights_other = swap(weights)
    bias_h = jnp.concatenate([hidden_bias, swap(hidden_bias)])
    noise = jnp.log(hidden_uniform) - jnp.log1p(-hidden_uniform)
    mine, others = cut(noise)
    noise_h = jnp.concatenate([mine, swap(others)], axis=1)
    noise = jnp.log(visible_uniform) - jnp.log1p(-visible_uniform)
    mine, others = cut(noise)
    noise_v = jnp.concatenate([mine, swap(others)], axis=0)

    def gather_col(array):
        both = jnp.concatenate([array, flip(array, "col", 8)], axis=0)
        return spread(both, "col", 2)

    def gather_row(array):
        all_zh = jnp.concatenate(spread(array, "row", 4), axis=0)
        return spread(all_zh, "row", 1)

    def sum_row(pieces):
        arrived = [pieces[0]] + [flip(pieces[s], "row", s) for s in (1, 2, 3)]
        partial = sum(a.astype(F32) for a in arrived)
        n = partial.shape[0] // 4
        part = [partial[i * n : (i + 1) * n] for i in range(4)]
        return part[0] + sum(flip(part[s].astype(BF16), "row", 4 * s).astype(F32) for s in (1, 2, 3))

    def sum_col(pieces):
        arrived = [pieces[0]] + [flip(pieces[s], "col", 2 * s) for s in (1, 2, 3)]
        partial = sum(a.astype(F32) for a in arrived)
        n = partial.shape[0] // 2
        return partial[:n] + flip(partial[n:].astype(BF16), "col", 8).astype(F32)

    def share(probs):
        return gather_row(jnp.concatenate([probs[:, :hiddens], swap(probs[:, hiddens:])], axis=0))

    visible_all = gather_col(visible)
    field_pos = sum_row(forward(q, visible_all, weights, weights_other)) + bias_h
    probs_pos = jax.nn.sigmoid(field_pos).astype(BF16)
    sample = jax.nn.sigmoid(2.0 * (field_pos + noise_h)).astype(BF16)
    sample_all = gather_row(sample)
    field_neg = sum_col(backward(q, sample_all, weights, weights_other)) + visible_bias
    recon = jax.nn.sigmoid(2.0 * (field_neg + noise_v)).astype(BF16)
    recon_all = gather_col(recon)
    field_back = sum_row(forward(q, recon_all, weights, weights_other)) + bias_h
    probs_neg = jax.nn.sigmoid(field_back).astype(BF16)

    grad_weights, grad_visible, grad_hidden = gradient(
        q,
        total,
        visible_all,
        [swap(a) for a in visible_all],
        recon_all,
        [swap(a) for a in recon_all],
        share(probs_pos),
        share(probs_neg),
    )
    hidden_sample = whole_block(sample[:, :hiddens], swap(sample[:, hiddens:]))
    reconstruction = whole_block(recon[:half], swap(recon[half:]))
    return (
        grad_weights,
        grad_visible.reshape(-1),
        grad_hidden.reshape(-1),
        hidden_sample,
        reconstruction,
    )


def solution(mesh):
    placed = (
        P("col", "row"),
        P("row", "col"),
        P("col", "row"),
        P("row", "col"),
        P("row"),
        P("col"),
    )
    return jax.shard_map(
        on_device,
        mesh=mesh,
        in_specs=placed,
        out_specs=(P("row", "col"), P("row"), P("col"), P("row", "col"), P("col", "row")),
        check_vma=False,
    )
```

```python
import functools

import jax
import jax.numpy as jnp
from jax import lax
from jax.experimental import pallas as pl
from jax.experimental.pallas import tpu as pltpu
from jax.sharding import PartitionSpec as P

F32, BF16 = jnp.float32, jnp.bfloat16


def flip(array, axis, bits):
    return lax.ppermute(array, axis, [(i, i ^ bits) for i in range(16)])


def spread(array, axis, step):
    return [array] + [flip(array, axis, s * step) for s in (1, 2, 3)]


def row_to_index(p):
    return (p & 3) * 4 + (p >> 2)


VMEM = pl.BlockSpec(memory_space=pltpu.VMEM)
SMEM = pl.BlockSpec(memory_space=pltpu.SMEM)
HBM = pl.BlockSpec(memory_space=pltpu.HBM)
PARAMS = pltpu.CompilerParams(vmem_limit_bytes=8 << 20)


def in_hbm(array):
    return pltpu.with_memory_space_constraint(array, pltpu.HBM)


def forward_kernel(q_ref, *refs):
    pieces, (own, other), outs = refs[:8], refs[8:10], refs[10:15]
    tiles, sems = refs[15:]
    (lhs, first, *sent) = outs
    width = own.shape[1]
    tile = tiles.shape[2]
    steps = width // tile
    copies = []
    for i in range(2 * steps):
        source = own if i < steps else other
        columns = pl.ds((i % steps) * tile, tile)
        copies.append(pltpu.make_async_copy(source.at[:, columns], tiles.at[i], sems.at[i]))
        copies[-1].start()
    q = q_ref[0]
    rows = pieces[0].shape[0] // 2
    for i, piece in enumerate(pieces):
        for core in range(2):
            place = row_to_index((i * 2 + core) ^ q)
            at = pl.ds(pl.multiple_of(place * rows, rows), rows)
            lhs[at, :] = piece[core * rows : (core + 1) * rows, :]
    n = first.shape[0]
    for i, copy in enumerate(copies):
        copy.wait()
        product = jnp.dot(lhs[...], tiles[i], preferred_element_type=F32)
        for j, out in enumerate((first, *sent)):
            out[:, i * tile : (i + 1) * tile] = product[j * n : (j + 1) * n].astype(out.dtype)


def backward_kernel(q_ref, *refs):
    pieces, (own, other), outs = refs[:4], refs[4:6], refs[6:14]
    lhs, tiles, sems = refs[14:]
    height, width = own.shape
    tile = tiles.shape[2]
    copies = []
    for i in range(height // tile):
        part = pl.ds(i * tile, tile)
        copies.append(
            [
                pltpu.make_async_copy(w.at[part, :], tiles.at[i, k], sems.at[i, k])
                for k, w in enumerate((own, other))
            ]
        )
        for copy in copies[-1]:
            copy.start()
    q = q_ref[0]
    rows = pieces[0].shape[0] // 4
    for x, piece in enumerate(pieces):
        for zh in range(4):
            at = pl.ds(pl.multiple_of(((zh * 4 + x) ^ q) * rows, rows), rows)
            lhs[at, :] = piece[zh * rows : (zh + 1) * rows, :]
    n = outs[0].shape[0]
    transposed = (((1,), (1,)), ((), ()))
    for i, pair in enumerate(copies):
        for copy in pair:
            copy.wait()
        product = lax.dot_general(
            lhs[:, :width], tiles[i, 0], transposed, preferred_element_type=F32
        ) + lax.dot_general(lhs[:, width:], tiles[i, 1], transposed, preferred_element_type=F32)
        for j, out in enumerate(outs):
            out[:, i * tile : (i + 1) * tile] = product[j * n : (j + 1) * n].astype(out.dtype)


def multiply(kernel, q, pieces, own, other, outs, scratch):
    n, depth = pieces[0].shape
    return pl.pallas_call(
        kernel,
        out_shape=outs,
        in_specs=[SMEM] + [VMEM] * len(pieces) + [HBM] * 2,
        out_specs=[VMEM] * len(outs),
        scratch_shapes=scratch,
        compiler_params=pltpu.CompilerParams(vmem_limit_bytes=16 << 20),
        cost_estimate=pl.CostEstimate(
            flops=4 * len(pieces) * n * own.size,
            bytes_accessed=4 * own.size + 4 * len(pieces) * n * depth,
            transcendentals=0,
        ),
    )(q, *pieces, in_hbm(own), in_hbm(other))


def forward(q, pieces, own, other, tile=512):
    n, depth = pieces[0].shape
    width = own.shape[1]
    lhs, first, *sent = multiply(
        forward_kernel,
        q,
        pieces,
        own,
        other,
        [jax.ShapeDtypeStruct((8 * n, depth), BF16), jax.ShapeDtypeStruct((2 * n, 2 * width), F32)]
        + [jax.ShapeDtypeStruct((2 * n, 2 * width), BF16)] * 3,
        [pltpu.VMEM((2 * width // tile, depth, tile), BF16), pltpu.SemaphoreType.DMA((2 * width // tile,))],
    )
    return lhs, first, sent


def backward(q, pieces, own, other, tile=512):
    n, depth = pieces[0].shape
    height, width = own.shape
    sent = [jax.ShapeDtypeStruct((n // 2, height), BF16)] * 3
    kept = [jax.ShapeDtypeStruct((n // 2, height), F32)]
    outs = multiply(
        backward_kernel,
        q,
        pieces,
        own,
        other,
        kept + sent + kept + sent,
        [
            pltpu.VMEM((4 * n, depth), BF16),
            pltpu.VMEM((height // tile, 2, tile, width), BF16),
            pltpu.SemaphoreType.DMA((height // tile, 2)),
        ],
    )
    return outs[0], outs[4], outs[1:4], outs[5:8]


def stack_kernel(*refs):
    positive, negative, out, sem = refs[:4], refs[4:8], refs[8], refs[9]
    halves, n = negative[0].shape[:2]
    copies = []
    for i in range(4):
        for half in range(halves):
            at = pl.ds((half * 4 + i) * n, n)
            copies.append(pltpu.make_async_copy(positive[i].at[half], out.at[at, :], sem.at[i, half]))
            copies[-1].start()
    for i in range(4):
        for half in range(halves):
            at = ((halves + half) * 4 + i) * n
            out[at : at + n, :] = -negative[i][half]
    for copy in copies:
        copy.wait()


def stack(positive, negative):
    halves, n, width = positive[0].shape
    return pl.pallas_call(
        stack_kernel,
        out_shape=jax.ShapeDtypeStruct((8 * halves * n, width), BF16),
        in_specs=[HBM] * 4 + [VMEM] * 4,
        out_specs=VMEM,
        scratch_shapes=[pltpu.SemaphoreType.DMA((4, halves))],
        compiler_params=PARAMS,
        cost_estimate=pl.CostEstimate(
            flops=0, bytes_accessed=32 * halves * n * width, transcendentals=0
        ),
    )(*(in_hbm(p) for p in positive), *negative)


def turn_kernel(*refs):
    *arrays, out = refs
    n, depth = arrays[0].shape
    tile = 256
    for i, ref in enumerate(arrays):
        for j in range(depth // tile):
            out[j * tile : (j + 1) * tile, i * n : (i + 1) * n] = ref[:, j * tile : (j + 1) * tile].T


def turn(arrays):
    n, depth = arrays[0].shape
    return pl.pallas_call(
        turn_kernel,
        out_shape=jax.ShapeDtypeStruct((depth, len(arrays) * n), BF16),
        in_specs=[VMEM] * len(arrays),
        out_specs=VMEM,
        compiler_params=pltpu.CompilerParams(vmem_limit_bytes=16 << 20),
        cost_estimate=pl.CostEstimate(
            flops=0, bytes_accessed=4 * len(arrays) * n * depth, transcendentals=0
        ),
    )(*arrays)


def after(array, *others):
    return lax.optimization_barrier((array, *others))[0]


def together(*groups):
    return lax.optimization_barrier(groups)


def on_device(visible_data, hidden_uniform, visible_uniform, weights, visible_bias, hidden_bias):
    row, col = lax.axis_index("row"), lax.axis_index("col")
    core = col & 1
    block = visible_data.shape[0]
    hiddens = weights.shape[1]
    half = block // 2
    total = block * 16
    q = (row ^ col).astype(jnp.int32).reshape(1)

    def halve(array):
        return (
            lax.dynamic_slice_in_dim(array, core * half, half, 0),
            lax.dynamic_slice_in_dim(array, (1 - core) * half, half, 0),
        )

    def swap(array):
        return flip(array, "col", 1)

    def whole_block(mine, others):
        first = jnp.where(core == 0, mine, others)
        return jnp.concatenate([first, jnp.where(core == 0, others, mine)], axis=0)

    def exchange(sent, axis, step):
        return [flip(a, axis, s * step) for s, a in zip((1, 2, 3), sent)]

    def total_of(own, arrived):
        return own.astype(F32) + sum(a.astype(F32) for a in arrived)

    def quarters(array):
        n = array.shape[0] // 4
        return [array[i * n : (i + 1) * n] for i in range(4)]

    def sum_zh(partial):
        parts = quarters(partial)
        return total_of(parts[0], exchange([p.astype(BF16) for p in parts[1:]], "row", 4))

    def from_zl_y(own):
        return spread(own, "col", 2) + spread(flip(own, "col", 8), "col", 2)

    def from_zh(pair):
        return jnp.concatenate(spread(pair, "row", 4), axis=1)

    mine, others = halve(visible_data)
    arrived = swap(others)
    visible = jnp.concatenate([mine, arrived], axis=0)
    weights_other = swap(after(weights, arrived))
    visible_lhs, own, sent = forward(q, from_zl_y(visible), weights, weights_other)

    sent, hidden_uniform, visible_uniform, bias = together(
        sent, hidden_uniform, visible_uniform, hidden_bias
    )
    arrived = exchange(sent, "row", 1)
    mine_h, others_h = halve(jnp.log(hidden_uniform) - jnp.log1p(-hidden_uniform))
    mine_v, others_v = halve(jnp.log(visible_uniform) - jnp.log1p(-visible_uniform))
    others = swap(
        jnp.concatenate(
            [others_h, *jnp.split(others_v, 2, axis=1), jnp.broadcast_to(bias, (8, hiddens))], axis=0
        )
    )
    noise_h = jnp.concatenate([mine_h, others[:half]], axis=1)
    others_v = jnp.concatenate([others[half : 2 * half], others[2 * half : 3 * half]], axis=1)
    noise_v = jnp.concatenate([mine_v, others_v], axis=0)
    bias_h = jnp.concatenate([hidden_bias, others[3 * half]])
    arrived, noise_h, noise_v, bias_h = together(arrived, noise_h, noise_v, bias_h)
    field_pos = sum_zh(total_of(own, arrived)) + bias_h
    probs_pos = jax.nn.sigmoid(field_pos).astype(BF16)
    sample = jax.nn.sigmoid(2.0 * (field_pos + noise_h)).astype(BF16)

    gathered = jnp.concatenate(spread(sample, "row", 4), axis=0)
    others = swap(jnp.concatenate([probs_pos[:, hiddens:], sample[:, hiddens:]], axis=0))
    pos = jnp.stack([probs_pos[:, :hiddens], others[:half]])
    hidden_sample = whole_block(sample[:, :hiddens], others[half:])
    gathered, pos = together(gathered, pos)
    pieces = spread(gathered, "row", 1)
    pos = from_zh(pos)
    pieces, pos = together(pieces, pos)
    own0, own1, sent0, sent1 = backward(q, pieces, weights, weights_other)

    sent0, sent1, pos = together(sent0, sent1, pos)
    arrived1 = exchange(sent1, "col", 2)
    arrived0 = exchange(sent0, "col", 2)
    pos = spread(pos, "row", 1)
    partial = total_of(own1, arrived1).astype(BF16)
    field_neg = total_of(own0, arrived0) + flip(partial, "col", 8).astype(F32) + visible_bias
    recon = jax.nn.sigmoid(2.0 * (field_neg + noise_v)).astype(BF16)

    recon, visible_own = together(recon, visible_lhs)
    pieces = from_zl_y(recon)
    visible_other = swap(visible_own)
    pieces, visible_other = together(pieces, visible_other)
    recon_lhs, own, sent = forward(q, pieces, weights, weights_other)

    sent, recon_own, pos = together(sent, recon_lhs, pos)
    arrived = exchange(sent, "row", 1)
    recon_other = swap(recon_own)
    partial = total_of(own, arrived)
    partial, recon_other = together(partial, recon_other)
    place = row_to_index(row ^ col) * half
    reconstruction = whole_block(
        recon[:half], lax.dynamic_slice_in_dim(recon_other, place, half, 0)
    )
    field_back = sum_zh(partial) + bias_h
    probs_neg = jax.nn.sigmoid(field_back).astype(BF16)
    turned = turn([visible_own, visible_other, recon_own, recon_other])
    grad_visible = (
        jnp.sum(visible_own.astype(F32) + visible_other.astype(F32), axis=0)
        - jnp.sum(recon_own.astype(F32) + recon_other.astype(F32), axis=0)
    ) / total

    pair = from_zh(jnp.stack([probs_neg[:, :hiddens], swap(probs_neg[:, hiddens:])]))
    pair, turned, grad_visible = together(pair, turned, grad_visible)
    right = stack(pos, spread(pair, "row", 1))
    grad_weights = (jnp.dot(turned, right, preferred_element_type=F32) / total).astype(BF16)
    grad_hidden = jnp.sum(right.astype(F32), axis=0) / total
    return (grad_weights, grad_visible, grad_hidden, hidden_sample, reconstruction)


def solution(mesh):
    placed = (
        P("col", "row"),
        P("row", "col"),
        P("col", "row"),
        P("row", "col"),
        P("row"),
        P("col"),
    )
    return jax.shard_map(
        on_device,
        mesh=mesh,
        in_specs=placed,
        out_specs=(P("row", "col"), P("row"), P("col"), P("row", "col"), P("col", "row")),
        check_vma=False,
    )
```

```python
import functools

import jax
import jax.numpy as jnp
from jax import lax
from jax.experimental import pallas as pl
from jax.experimental.pallas import tpu as pltpu
from jax.sharding import PartitionSpec as P

F32, BF16 = jnp.float32, jnp.bfloat16


def flip(array, axis, bits):
    return lax.ppermute(array, axis, [(i, i ^ bits) for i in range(16)])


def spread(array, axis, step):
    return [array] + [flip(array, axis, s * step) for s in (1, 3, 2)]


def gray(v):
    return v ^ ((v >> 1) & 5)


def row_to_index(p):
    return (gray(p) & 3) * 4 + (gray(p) >> 2)


VMEM = pl.BlockSpec(memory_space=pltpu.VMEM)
SMEM = pl.BlockSpec(memory_space=pltpu.SMEM)
HBM = pl.BlockSpec(memory_space=pltpu.HBM)
PARAMS = pltpu.CompilerParams(vmem_limit_bytes=8 << 20)


def in_hbm(array):
    return pltpu.with_memory_space_constraint(array, pltpu.HBM)


def forward_kernel(q_ref, *refs):
    pieces, (own, other), outs = refs[:8], refs[8:10], refs[10:15]
    tiles, sems = refs[15:]
    (lhs, first, *sent) = outs
    width = own.shape[1]
    tile = tiles.shape[2]
    steps = width // tile
    copies = []
    for i in range(2 * steps):
        source = own if i < steps else other
        columns = pl.ds((i % steps) * tile, tile)
        copies.append(pltpu.make_async_copy(source.at[:, columns], tiles.at[i], sems.at[i]))
        copies[-1].start()
    q = q_ref[0]
    rows = pieces[0].shape[0] // 2
    for i, piece in enumerate(pieces):
        for core in range(2):
            place = row_to_index(((i >> 2) * 8 + gray(i & 3) * 2 + core) ^ q)
            at = pl.ds(pl.multiple_of(place * rows, rows), rows)
            lhs[at, :] = piece[core * rows : (core + 1) * rows, :]
    n = first.shape[0]
    for i, copy in enumerate(copies):
        copy.wait()
        product = jnp.dot(lhs[...], tiles[i], preferred_element_type=F32)
        for j, out in enumerate((first, *sent)):
            out[:, i * tile : (i + 1) * tile] = product[j * n : (j + 1) * n].astype(out.dtype)


def backward_kernel(q_ref, *refs):
    pieces, (own, other), outs = refs[:4], refs[4:6], refs[6:14]
    lhs, tiles, sems = refs[14:]
    height, width = own.shape
    tile = tiles.shape[2]
    copies = []
    for i in range(height // tile):
        part = pl.ds(i * tile, tile)
        copies.append(
            [
                pltpu.make_async_copy(w.at[part, :], tiles.at[i, k], sems.at[i, k])
                for k, w in enumerate((own, other))
            ]
        )
        for copy in copies[-1]:
            copy.start()
    q = q_ref[0]
    rows = pieces[0].shape[0] // 4
    for x, piece in enumerate(pieces):
        for zh in range(4):
            block = (gray(zh) * 4 + gray(x)) ^ q
            place = (block & 8) + gray((block >> 1) & 3) * 2 + (block & 1)
            at = pl.ds(pl.multiple_of(place * rows, rows), rows)
            lhs[at, :] = piece[zh * rows : (zh + 1) * rows, :]
    n = outs[0].shape[0]
    transposed = (((1,), (1,)), ((), ()))
    for i, pair in enumerate(copies):
        for copy in pair:
            copy.wait()
        product = lax.dot_general(
            lhs[:, :width], tiles[i, 0], transposed, preferred_element_type=F32
        ) + lax.dot_general(lhs[:, width:], tiles[i, 1], transposed, preferred_element_type=F32)
        for j, out in enumerate(outs):
            out[:, i * tile : (i + 1) * tile] = product[j * n : (j + 1) * n].astype(out.dtype)


def multiply(kernel, q, pieces, own, other, outs, scratch):
    n, depth = pieces[0].shape
    return pl.pallas_call(
        kernel,
        out_shape=outs,
        in_specs=[SMEM] + [VMEM] * len(pieces) + [HBM] * 2,
        out_specs=[VMEM] * len(outs),
        scratch_shapes=scratch,
        compiler_params=pltpu.CompilerParams(vmem_limit_bytes=16 << 20),
        cost_estimate=pl.CostEstimate(
            flops=4 * len(pieces) * n * own.size,
            bytes_accessed=4 * own.size + 4 * len(pieces) * n * depth,
            transcendentals=0,
        ),
    )(q, *pieces, in_hbm(own), in_hbm(other))


def forward(q, pieces, own, other, tile=512):
    n, depth = pieces[0].shape
    width = own.shape[1]
    lhs, first, *sent = multiply(
        forward_kernel,
        q,
        pieces,
        own,
        other,
        [jax.ShapeDtypeStruct((8 * n, depth), BF16), jax.ShapeDtypeStruct((2 * n, 2 * width), BF16)]
        + [jax.ShapeDtypeStruct((2 * n, 2 * width), BF16)] * 3,
        [pltpu.VMEM((2 * width // tile, depth, tile), BF16), pltpu.SemaphoreType.DMA((2 * width // tile,))],
    )
    return lhs, first, sent


def backward(q, pieces, own, other, tile=512):
    n, depth = pieces[0].shape
    height, width = own.shape
    sent = [jax.ShapeDtypeStruct((n // 2, height), BF16)] * 3
    kept = [jax.ShapeDtypeStruct((n // 2, height), BF16)]
    outs = multiply(
        backward_kernel,
        q,
        pieces,
        own,
        other,
        kept + sent + kept + sent,
        [
            pltpu.VMEM((4 * n, depth), BF16),
            pltpu.VMEM((height // tile, 2, tile, width), BF16),
            pltpu.SemaphoreType.DMA((height // tile, 2)),
        ],
    )
    return outs[0], outs[4], outs[1:4], outs[5:8]


def stack_kernel(*refs):
    positive, negative, out, sem = refs[:2], refs[2:6], refs[6], refs[7]
    copies = []
    halves, n = positive[0].shape[:2]
    for i, piece in enumerate(positive):
        for half in range(halves):
            at = pl.ds((half * 2 + i) * n, n)
            copies.append(pltpu.make_async_copy(piece.at[half], out.at[at, :], sem.at[i, half]))
            copies[-1].start()
    n = negative[0].shape[1]
    for i, piece in enumerate(negative):
        for half in range(halves):
            at = ((halves + half) * 4 + i) * n
            out[at : at + n, :] = -piece[half]
    for copy in copies:
        copy.wait()


def stack(positive, negative):
    halves, n, width = negative[0].shape
    return pl.pallas_call(
        stack_kernel,
        out_shape=jax.ShapeDtypeStruct((8 * halves * n, width), BF16),
        in_specs=[HBM] * 2 + [VMEM] * 4,
        out_specs=VMEM,
        scratch_shapes=[pltpu.SemaphoreType.DMA((2, halves))],
        compiler_params=PARAMS,
        cost_estimate=pl.CostEstimate(
            flops=0, bytes_accessed=32 * halves * n * width, transcendentals=0
        ),
    )(*(in_hbm(p) for p in positive), *negative)


def turn_kernel(*refs):
    *arrays, out = refs
    n, depth = arrays[0].shape
    tile = 256
    for i, ref in enumerate(arrays):
        for j in range(depth // tile):
            out[j * tile : (j + 1) * tile, i * n : (i + 1) * n] = ref[:, j * tile : (j + 1) * tile].T


def turn(arrays):
    n, depth = arrays[0].shape
    return pl.pallas_call(
        turn_kernel,
        out_shape=jax.ShapeDtypeStruct((depth, len(arrays) * n), BF16),
        in_specs=[VMEM] * len(arrays),
        out_specs=VMEM,
        compiler_params=pltpu.CompilerParams(vmem_limit_bytes=16 << 20),
        cost_estimate=pl.CostEstimate(
            flops=0, bytes_accessed=4 * len(arrays) * n * depth, transcendentals=0
        ),
    )(*arrays)


def after(array, *others):
    return lax.optimization_barrier((array, *others))[0]


def together(*groups):
    return lax.optimization_barrier(groups)


def on_device(visible_data, hidden_uniform, visible_uniform, weights, visible_bias, hidden_bias):
    row, col = lax.axis_index("row"), lax.axis_index("col")
    core = col & 1
    block = visible_data.shape[0]
    hiddens = weights.shape[1]
    half = block // 2
    total = block * 16
    q = (row ^ col).astype(jnp.int32).reshape(1)

    def halve(array):
        return (
            lax.dynamic_slice_in_dim(array, core * half, half, 0),
            lax.dynamic_slice_in_dim(array, (1 - core) * half, half, 0),
        )

    def swap(array):
        return flip(array, "col", 1)

    def whole_block(mine, others):
        first = jnp.where(core == 0, mine, others)
        return jnp.concatenate([first, jnp.where(core == 0, others, mine)], axis=0)

    def exchange(sent, axis, step):
        return [flip(a, axis, s * step) for s, a in zip((1, 3, 2), sent)]

    def total_of(own, arrived):
        return own.astype(F32) + sum(a.astype(F32) for a in arrived)

    def quarters(array):
        n = array.shape[0] // 4
        return [array[i * n : (i + 1) * n] for i in range(4)]

    def doubled(array, distance):
        return jnp.concatenate([array, flip(array, "row", distance)], axis=1)

    def sum_zh(partial):
        parts = quarters(partial)
        return total_of(parts[0], exchange([p.astype(BF16) for p in parts[1:]], "row", 4))

    def from_zl_y(own):
        return spread(own, "col", 2) + spread(flip(own, "col", 8), "col", 2)

    def from_zh(pair):
        return jnp.concatenate(spread(pair, "row", 4), axis=1)

    mine, others = halve(visible_data)
    arrived = swap(others)
    visible = jnp.concatenate([mine, arrived], axis=0)
    weights_other = swap(after(weights, arrived))
    visible_lhs, own, sent = forward(q, from_zl_y(visible), weights, weights_other)

    sent, hidden_uniform, visible_uniform, bias = together(
        sent, hidden_uniform, visible_uniform, hidden_bias
    )
    arrived = exchange(sent, "row", 1)
    mine_h, others_h = halve(jnp.log(hidden_uniform) - jnp.log1p(-hidden_uniform))
    mine_v, others_v = halve(jnp.log(visible_uniform) - jnp.log1p(-visible_uniform))
    others = swap(
        jnp.concatenate(
            [others_h, *jnp.split(others_v, 2, axis=1), jnp.broadcast_to(bias, (8, hiddens))], axis=0
        )
    )
    noise_h = jnp.concatenate([mine_h, others[:half]], axis=1)
    others_v = jnp.concatenate([others[half : 2 * half], others[2 * half : 3 * half]], axis=1)
    noise_v = jnp.concatenate([mine_v, others_v], axis=0)
    bias_h = jnp.concatenate([hidden_bias, others[3 * half]])
    arrived, noise_h, noise_v, bias_h = together(arrived, noise_h, noise_v, bias_h)
    field_pos = sum_zh(total_of(own, arrived)) + bias_h
    probs_pos = jax.nn.sigmoid(field_pos).astype(BF16)
    sample = jax.nn.sigmoid(2.0 * (field_pos + noise_h)).astype(BF16)

    gathered = jnp.concatenate(spread(sample, "row", 4), axis=0)
    others = swap(jnp.concatenate([probs_pos[:, hiddens:], sample[:, hiddens:]], axis=0))
    pos = jnp.stack([probs_pos[:, :hiddens], others[:half]])
    hidden_sample = whole_block(sample[:, :hiddens], others[half:])
    gathered, pos = together(gathered, pos)
    pieces = spread(gathered, "row", 1)
    pos = doubled(pos, 4)
    pieces, pos = together(pieces, pos)
    own0, own1, sent0, sent1 = backward(q, pieces, weights, weights_other)

    sent0, sent1, pos = together(sent0, sent1, pos)
    arrived1 = exchange(sent1, "col", 2)
    arrived0 = exchange(sent0, "col", 2)
    pos = doubled(pos, 12)
    partial = total_of(own1, arrived1).astype(BF16)
    field_neg = total_of(own0, arrived0) + flip(partial, "col", 8).astype(F32) + visible_bias
    recon = jax.nn.sigmoid(2.0 * (field_neg + noise_v)).astype(BF16)

    recon, visible_own, pos = together(recon, visible_lhs, pos)
    pieces = from_zl_y(recon)
    pos = doubled(pos, 1)
    visible_other = swap(visible_own)
    pieces, visible_other, pos = together(pieces, visible_other, pos)
    recon_lhs, own, sent = forward(q, pieces, weights, weights_other)

    sent, recon_own = together(sent, recon_lhs)
    arrived = exchange(sent, "row", 1)
    recon_other = swap(recon_own)
    partial = total_of(own, arrived)
    partial, recon_other, pos = together(partial, recon_other, pos)
    pos = [pos, flip(pos, "row", 3)]
    field_back = sum_zh(partial) + bias_h
    probs_neg = jax.nn.sigmoid(field_back).astype(BF16)

    pair = from_zh(jnp.stack([probs_neg[:, :hiddens], swap(probs_neg[:, hiddens:])]))
    pair, pos, visible_own, visible_other, recon_own, recon_other, recon = together(
        pair, pos, visible_own, visible_other, recon_own, recon_other, recon
    )
    neg = spread(pair, "row", 1)
    turned = turn([visible_own, visible_other, recon_own, recon_other])
    grad_visible = (
        jnp.sum(visible_own.astype(F32) + visible_other.astype(F32), axis=0)
        - jnp.sum(recon_own.astype(F32) + recon_other.astype(F32), axis=0)
    ) / total
    place = row_to_index(row ^ col) * half
    reconstruction = whole_block(
        recon[:half], lax.dynamic_slice_in_dim(recon_other, place, half, 0)
    )
    neg, turned, grad_visible, reconstruction = together(neg, turned, grad_visible, reconstruction)
    right = stack(pos, neg)
    grad_weights = (jnp.dot(turned, right, preferred_element_type=F32) / total).astype(BF16)
    grad_hidden = jnp.sum(right.astype(F32) / total, axis=0)
    return (grad_weights, grad_visible, grad_hidden, hidden_sample, reconstruction)


def solution(mesh):
    placed = (
        P("col", "row"),
        P("row", "col"),
        P("col", "row"),
        P("row", "col"),
        P("row"),
        P("col"),
    )
    return jax.shard_map(
        on_device,
        mesh=mesh,
        in_specs=placed,
        out_specs=(P("row", "col"), P("row"), P("col"), P("row", "col"), P("col", "row")),
        check_vma=False,
    )
```

```python
import functools

import jax
import jax.numpy as jnp
from jax import lax
from jax.experimental import pallas as pl
from jax.experimental.pallas import tpu as pltpu
from jax.sharding import PartitionSpec as P

F32, BF16 = jnp.float32, jnp.bfloat16


def flip(array, axis, bits):
    return lax.ppermute(array, axis, [(i, i ^ bits) for i in range(16)])


def spread(array, axis, step):
    return [array] + [flip(array, axis, s * step) for s in (1, 3, 2)]


def gray(v):
    return v ^ ((v >> 1) & 5)


def row_to_index(p):
    return (gray(p) & 3) * 4 + (gray(p) >> 2)


VMEM = pl.BlockSpec(memory_space=pltpu.VMEM)
SMEM = pl.BlockSpec(memory_space=pltpu.SMEM)
HBM = pl.BlockSpec(memory_space=pltpu.HBM)
PARAMS = pltpu.CompilerParams(vmem_limit_bytes=8 << 20)


def in_hbm(array):
    return pltpu.with_memory_space_constraint(array, pltpu.HBM)


def forward_kernel(q_ref, *refs):
    pieces, (own, other), outs = refs[:8], refs[8:10], refs[10:15]
    tiles, sems = refs[15:]
    (lhs, first, *sent) = outs
    width = own.shape[1]
    tile = tiles.shape[2]
    steps = width // tile
    copies = []
    for i in range(2 * steps):
        source = own if i < steps else other
        columns = pl.ds((i % steps) * tile, tile)
        copies.append(pltpu.make_async_copy(source.at[:, columns], tiles.at[i], sems.at[i]))
        copies[-1].start()
    q = q_ref[0]
    rows = pieces[0].shape[0] // 2
    for i, piece in enumerate(pieces):
        for core in range(2):
            place = row_to_index(((i >> 2) * 8 + gray(i & 3) * 2 + core) ^ q)
            at = pl.ds(pl.multiple_of(place * rows, rows), rows)
            lhs[at, :] = piece[core * rows : (core + 1) * rows, :]
    n = first.shape[0]
    for i, copy in enumerate(copies):
        copy.wait()
        product = jnp.dot(lhs[...], tiles[i], preferred_element_type=F32)
        for j, out in enumerate((first, *sent)):
            out[:, i * tile : (i + 1) * tile] = product[j * n : (j + 1) * n].astype(out.dtype)


def backward_kernel(q_ref, *refs):
    pieces, (own, other), outs = refs[:4], refs[4:6], refs[6:14]
    lhs, tiles, sems = refs[14:]
    height, width = own.shape
    tile = tiles.shape[2]
    copies = []
    for i in range(height // tile):
        part = pl.ds(i * tile, tile)
        copies.append(
            [
                pltpu.make_async_copy(w.at[part, :], tiles.at[i, k], sems.at[i, k])
                for k, w in enumerate((own, other))
            ]
        )
        for copy in copies[-1]:
            copy.start()
    q = q_ref[0]
    rows = pieces[0].shape[0] // 4
    for x, piece in enumerate(pieces):
        for zh in range(4):
            block = (gray(zh) * 4 + gray(x)) ^ q
            place = (block & 8) + gray((block >> 1) & 3) * 2 + (block & 1)
            at = pl.ds(pl.multiple_of(place * rows, rows), rows)
            lhs[at, :] = piece[zh * rows : (zh + 1) * rows, :]
    n = outs[0].shape[0]
    transposed = (((1,), (1,)), ((), ()))
    for i, pair in enumerate(copies):
        for copy in pair:
            copy.wait()
        product = lax.dot_general(
            lhs[:, :width], tiles[i, 0], transposed, preferred_element_type=F32
        ) + lax.dot_general(lhs[:, width:], tiles[i, 1], transposed, preferred_element_type=F32)
        for j, out in enumerate(outs):
            out[:, i * tile : (i + 1) * tile] = product[j * n : (j + 1) * n].astype(out.dtype)


def multiply(kernel, q, pieces, own, other, outs, scratch):
    n, depth = pieces[0].shape
    return pl.pallas_call(
        kernel,
        out_shape=outs,
        in_specs=[SMEM] + [VMEM] * len(pieces) + [HBM] * 2,
        out_specs=[VMEM] * len(outs),
        scratch_shapes=scratch,
        compiler_params=pltpu.CompilerParams(vmem_limit_bytes=16 << 20),
        cost_estimate=pl.CostEstimate(
            flops=4 * len(pieces) * n * own.size,
            bytes_accessed=4 * own.size + 4 * len(pieces) * n * depth,
            transcendentals=0,
        ),
    )(q, *pieces, in_hbm(own), in_hbm(other))


def forward(q, pieces, own, other, tile=512):
    n, depth = pieces[0].shape
    width = own.shape[1]
    lhs, first, *sent = multiply(
        forward_kernel,
        q,
        pieces,
        own,
        other,
        [jax.ShapeDtypeStruct((8 * n, depth), BF16), jax.ShapeDtypeStruct((2 * n, 2 * width), BF16)]
        + [jax.ShapeDtypeStruct((2 * n, 2 * width), BF16)] * 3,
        [pltpu.VMEM((2 * width // tile, depth, tile), BF16), pltpu.SemaphoreType.DMA((2 * width // tile,))],
    )
    return lhs, first, sent


def backward(q, pieces, own, other, tile=512):
    n, depth = pieces[0].shape
    height, width = own.shape
    sent = [jax.ShapeDtypeStruct((n // 2, height), BF16)] * 3
    kept = [jax.ShapeDtypeStruct((n // 2, height), BF16)]
    outs = multiply(
        backward_kernel,
        q,
        pieces,
        own,
        other,
        kept + sent + kept + sent,
        [
            pltpu.VMEM((4 * n, depth), BF16),
            pltpu.VMEM((height // tile, 2, tile, width), BF16),
            pltpu.SemaphoreType.DMA((height // tile, 2)),
        ],
    )
    return outs[0], outs[4], outs[1:4], outs[5:8]


def stack_kernel(*refs):
    positive, negative, (out, sums, sem) = refs[:2], refs[2:6], refs[6:]
    copies = []
    halves, n = positive[0].shape[:2]
    for i, piece in enumerate(positive):
        for half in range(halves):
            at = pl.ds((half * 2 + i) * n, n)
            copies.append(pltpu.make_async_copy(piece.at[half], out.at[at, :], sem.at[i, half]))
            copies[-1].start()
    n = negative[0].shape[1]
    for i, piece in enumerate(negative):
        for half in range(halves):
            at = ((halves + half) * 4 + i) * n
            out[at : at + n, :] = -piece[half]
    for copy in copies:
        copy.wait()
    sums[...] = jnp.sum(out[...].astype(F32), axis=0, keepdims=True) / out.shape[0] * 2


def stack(positive, negative):
    halves, n, width = negative[0].shape
    return pl.pallas_call(
        stack_kernel,
        out_shape=[
            jax.ShapeDtypeStruct((8 * halves * n, width), BF16),
            jax.ShapeDtypeStruct((1, width), F32),
        ],
        in_specs=[HBM] * 2 + [VMEM] * 4,
        out_specs=[VMEM] * 2,
        scratch_shapes=[pltpu.SemaphoreType.DMA((2, halves))],
        compiler_params=PARAMS,
        cost_estimate=pl.CostEstimate(
            flops=0, bytes_accessed=32 * halves * n * width, transcendentals=0
        ),
    )(*(in_hbm(p) for p in positive), *negative)


def turn_kernel(*refs):
    *arrays, out = refs
    n, depth = arrays[0].shape
    tile = 256
    for i, ref in enumerate(arrays):
        for j in range(depth // tile):
            out[j * tile : (j + 1) * tile, i * n : (i + 1) * n] = ref[:, j * tile : (j + 1) * tile].T


def turn(arrays):
    n, depth = arrays[0].shape
    return pl.pallas_call(
        turn_kernel,
        out_shape=jax.ShapeDtypeStruct((depth, len(arrays) * n), BF16),
        in_specs=[VMEM] * len(arrays),
        out_specs=VMEM,
        compiler_params=pltpu.CompilerParams(vmem_limit_bytes=16 << 20),
        cost_estimate=pl.CostEstimate(
            flops=0, bytes_accessed=4 * len(arrays) * n * depth, transcendentals=0
        ),
    )(*arrays)


def after(array, *others):
    return lax.optimization_barrier((array, *others))[0]


def together(*groups):
    return lax.optimization_barrier(groups)


def on_device(visible_data, hidden_uniform, visible_uniform, weights, visible_bias, hidden_bias):
    row, col = lax.axis_index("row"), lax.axis_index("col")
    core = col & 1
    block = visible_data.shape[0]
    hiddens = weights.shape[1]
    half = block // 2
    total = block * 16
    q = (row ^ col).astype(jnp.int32).reshape(1)

    def halve(array):
        return (
            lax.dynamic_slice_in_dim(array, core * half, half, 0),
            lax.dynamic_slice_in_dim(array, (1 - core) * half, half, 0),
        )

    def swap(array):
        return flip(array, "col", 1)

    def whole_block(mine, others):
        first = jnp.where(core == 0, mine, others)
        return jnp.concatenate([first, jnp.where(core == 0, others, mine)], axis=0)

    def exchange(sent, axis, step):
        return [flip(a, axis, s * step) for s, a in zip((1, 3, 2), sent)]

    def total_of(own, arrived):
        return own.astype(F32) + sum(a.astype(F32) for a in arrived)

    def quarters(array):
        n = array.shape[0] // 4
        return [array[i * n : (i + 1) * n] for i in range(4)]

    def doubled(array, distance):
        return jnp.concatenate([array, flip(array, "row", distance)], axis=1)

    def sum_zh(partial):
        parts = quarters(partial)
        return total_of(parts[0], exchange([p.astype(BF16) for p in parts[1:]], "row", 4))

    def from_zl_y(own):
        return spread(own, "col", 2) + spread(flip(own, "col", 8), "col", 2)

    def from_zh(pair):
        return jnp.concatenate(spread(pair, "row", 4), axis=1)

    mine, others = halve(visible_data)
    arrived = swap(others)
    visible = jnp.concatenate([mine, arrived], axis=0)
    weights_other = swap(after(weights, arrived))
    visible_lhs, own, sent = forward(q, from_zl_y(visible), weights, weights_other)

    sent, visible_own, hidden_uniform, visible_uniform, bias = together(
        sent, visible_lhs, hidden_uniform, visible_uniform, hidden_bias
    )
    arrived = exchange(sent, "row", 1)
    visible_other = swap(visible_own)
    mine_h, others_h = halve(jnp.log(hidden_uniform) - jnp.log1p(-hidden_uniform))
    mine_v, others_v = halve(jnp.log(visible_uniform) - jnp.log1p(-visible_uniform))
    others = swap(
        jnp.concatenate(
            [others_h, *jnp.split(others_v, 2, axis=1), jnp.broadcast_to(bias, (8, hiddens))], axis=0
        )
    )
    noise_h = jnp.concatenate([mine_h, others[:half]], axis=1)
    others_v = jnp.concatenate([others[half : 2 * half], others[2 * half : 3 * half]], axis=1)
    noise_v = jnp.concatenate([mine_v, others_v], axis=0)
    bias_h = jnp.concatenate([hidden_bias, others[3 * half]])
    arrived, visible_other, noise_h, noise_v, bias_h = together(
        arrived, visible_other, noise_h, noise_v, bias_h
    )
    field_pos = sum_zh(total_of(own, arrived)) + bias_h
    probs_pos = jax.nn.sigmoid(field_pos).astype(BF16)
    sample = jax.nn.sigmoid(2.0 * (field_pos + noise_h)).astype(BF16)

    gathered = jnp.concatenate(spread(sample, "row", 4), axis=0)
    gathered, probs_pos, sample = together(gathered, probs_pos, sample)
    pieces = spread(gathered, "row", 1)
    others = swap(jnp.concatenate([probs_pos[:, hiddens:], sample[:, hiddens:]], axis=0))
    pos = jnp.stack([probs_pos[:, :hiddens], others[:half]])
    hidden_sample = whole_block(sample[:, :hiddens], others[half:])
    pos = doubled(pos, 4)
    pieces, pos = together(pieces, pos)
    own0, own1, sent0, sent1 = backward(q, pieces, weights, weights_other)

    sent0, sent1, pos = together(sent0, sent1, pos)
    arrived1 = exchange(sent1, "col", 2)
    arrived0 = exchange(sent0, "col", 2)
    pos = doubled(pos, 12)
    partial = total_of(own1, arrived1).astype(BF16)
    field_neg = total_of(own0, arrived0) + flip(partial, "col", 8).astype(F32) + visible_bias
    recon = jax.nn.sigmoid(2.0 * (field_neg + noise_v)).astype(BF16)

    recon, pos = together(recon, pos)
    pieces = from_zl_y(recon)
    pos = doubled(pos, 1)
    pieces, pos = together(pieces, pos)
    recon_lhs, own, sent = forward(q, pieces, weights, weights_other)

    sent, recon_own = together(sent, recon_lhs)
    arrived = exchange(sent, "row", 1)
    recon_other = swap(recon_own)
    partial = total_of(own, arrived)
    partial, recon_other, pos = together(partial, recon_other, pos)
    pos = [pos, flip(pos, "row", 3)]
    field_back = sum_zh(partial) + bias_h
    probs_neg = jax.nn.sigmoid(field_back).astype(BF16)

    pair = from_zh(jnp.stack([probs_neg[:, :hiddens], swap(probs_neg[:, hiddens:])]))
    pair, pos, visible_own, visible_other, recon_own, recon_other, recon = together(
        pair, pos, visible_own, visible_other, recon_own, recon_other, recon
    )
    neg = spread(pair, "row", 1)
    turned = turn([visible_own, visible_other, recon_own, recon_other])
    grad_visible = (
        jnp.sum(visible_own.astype(F32) + visible_other.astype(F32), axis=0)
        - jnp.sum(recon_own.astype(F32) + recon_other.astype(F32), axis=0)
    ) / total
    place = row_to_index(row ^ col) * half
    reconstruction = whole_block(
        recon[:half], lax.dynamic_slice_in_dim(recon_other, place, half, 0)
    )
    neg, turned, grad_visible, reconstruction = together(neg, turned, grad_visible, reconstruction)
    right, grad_hidden = stack(pos, neg)
    grad_weights = (jnp.dot(turned, right, preferred_element_type=F32) / total).astype(BF16)
    return (grad_weights, grad_visible, grad_hidden.reshape(-1), hidden_sample, reconstruction)


def solution(mesh):
    placed = (
        P("col", "row"),
        P("row", "col"),
        P("col", "row"),
        P("row", "col"),
        P("row"),
        P("col"),
    )
    return jax.shard_map(
        on_device,
        mesh=mesh,
        in_specs=placed,
        out_specs=(P("row", "col"), P("row"), P("col"), P("row", "col"), P("col", "row")),
        check_vma=False,
    )
```

```python
import functools

import jax
import jax.numpy as jnp
from jax import lax
from jax.experimental import pallas as pl
from jax.experimental.pallas import tpu as pltpu
from jax.sharding import PartitionSpec as P

F32, BF16 = jnp.float32, jnp.bfloat16


def flip(array, axis, bits):
    return lax.ppermute(array, axis, [(i, i ^ bits) for i in range(16)])


def spread(array, axis, step):
    return [array] + [flip(array, axis, s * step) for s in (1, 3, 2)]


def gray(v):
    return v ^ ((v >> 1) & 5)


def row_to_index(p):
    return (gray(p) & 3) * 4 + (gray(p) >> 2)


VMEM = pl.BlockSpec(memory_space=pltpu.VMEM)
SMEM = pl.BlockSpec(memory_space=pltpu.SMEM)
HBM = pl.BlockSpec(memory_space=pltpu.HBM)
PARAMS = pltpu.CompilerParams(vmem_limit_bytes=8 << 20)


def in_hbm(array):
    return pltpu.with_memory_space_constraint(array, pltpu.HBM)


def forward_kernel(q_ref, *refs):
    pieces, (own, other), outs = refs[:8], refs[8:10], refs[10:15]
    tiles, sems = refs[15:]
    (lhs, first, *sent) = outs
    width = own.shape[1]
    tile = tiles.shape[2]
    steps = width // tile
    copies = []
    for i in range(2 * steps):
        source = own if i < steps else other
        columns = pl.ds((i % steps) * tile, tile)
        copies.append(pltpu.make_async_copy(source.at[:, columns], tiles.at[i], sems.at[i]))
        copies[-1].start()
    q = q_ref[0]
    rows = pieces[0].shape[0] // 2
    for i, piece in enumerate(pieces):
        for core in range(2):
            place = row_to_index(((i >> 2) * 8 + gray(i & 3) * 2 + core) ^ q)
            at = pl.ds(pl.multiple_of(place * rows, rows), rows)
            lhs[at, :] = piece[core * rows : (core + 1) * rows, :]
    n = first.shape[0]
    for i, copy in enumerate(copies):
        copy.wait()
        product = jnp.dot(lhs[...], tiles[i], preferred_element_type=F32)
        for j, out in enumerate((first, *sent)):
            out[:, i * tile : (i + 1) * tile] = product[j * n : (j + 1) * n].astype(out.dtype)


def backward_kernel(q_ref, *refs):
    pieces, (own, other), outs = refs[:4], refs[4:6], refs[6:14]
    lhs, tiles, sems = refs[14:]
    height, width = own.shape
    tile = tiles.shape[2]
    copies = []
    for i in range(height // tile):
        part = pl.ds(i * tile, tile)
        copies.append(
            [
                pltpu.make_async_copy(w.at[part, :], tiles.at[i, k], sems.at[i, k])
                for k, w in enumerate((own, other))
            ]
        )
        for copy in copies[-1]:
            copy.start()
    q = q_ref[0]
    rows = pieces[0].shape[0] // 4
    for x, piece in enumerate(pieces):
        for zh in range(4):
            block = (gray(zh) * 4 + gray(x)) ^ q
            place = (block & 8) + gray((block >> 1) & 3) * 2 + (block & 1)
            at = pl.ds(pl.multiple_of(place * rows, rows), rows)
            lhs[at, :] = piece[zh * rows : (zh + 1) * rows, :]
    n = outs[0].shape[0]
    transposed = (((1,), (1,)), ((), ()))
    for i, pair in enumerate(copies):
        for copy in pair:
            copy.wait()
        product = lax.dot_general(
            lhs[:, :width], tiles[i, 0], transposed, preferred_element_type=F32
        ) + lax.dot_general(lhs[:, width:], tiles[i, 1], transposed, preferred_element_type=F32)
        for j, out in enumerate(outs):
            out[:, i * tile : (i + 1) * tile] = product[j * n : (j + 1) * n].astype(out.dtype)


def multiply(kernel, q, pieces, own, other, outs, scratch):
    n, depth = pieces[0].shape
    return pl.pallas_call(
        kernel,
        out_shape=outs,
        in_specs=[SMEM] + [VMEM] * len(pieces) + [HBM] * 2,
        out_specs=[VMEM] * len(outs),
        scratch_shapes=scratch,
        compiler_params=pltpu.CompilerParams(vmem_limit_bytes=16 << 20),
        cost_estimate=pl.CostEstimate(
            flops=4 * len(pieces) * n * own.size,
            bytes_accessed=4 * own.size + 4 * len(pieces) * n * depth,
            transcendentals=0,
        ),
    )(q, *pieces, in_hbm(own), in_hbm(other))


def forward(q, pieces, own, other, tile=512):
    n, depth = pieces[0].shape
    width = own.shape[1]
    lhs, first, *sent = multiply(
        forward_kernel,
        q,
        pieces,
        own,
        other,
        [jax.ShapeDtypeStruct((8 * n, depth), BF16), jax.ShapeDtypeStruct((2 * n, 2 * width), BF16)]
        + [jax.ShapeDtypeStruct((2 * n, 2 * width), BF16)] * 3,
        [pltpu.VMEM((2 * width // tile, depth, tile), BF16), pltpu.SemaphoreType.DMA((2 * width // tile,))],
    )
    return lhs, first, sent


def backward(q, pieces, own, other, tile=512):
    n, depth = pieces[0].shape
    height, width = own.shape
    sent = [jax.ShapeDtypeStruct((n // 2, height), BF16)] * 3
    kept = [jax.ShapeDtypeStruct((n // 2, height), BF16)]
    outs = multiply(
        backward_kernel,
        q,
        pieces,
        own,
        other,
        kept + sent + kept + sent,
        [
            pltpu.VMEM((4 * n, depth), BF16),
            pltpu.VMEM((height // tile, 2, tile, width), BF16),
            pltpu.SemaphoreType.DMA((height // tile, 2)),
        ],
    )
    return outs[0], outs[4], outs[1:4], outs[5:8]


ANY = pl.BlockSpec(memory_space=pl.ANY)


def place_kernel(first, count, *refs):
    pieces, (out, sums, sem) = refs[-3 - count : -3], refs[-3:]
    halves, n = pieces[0].shape[:2]
    copies = []
    for half in range(halves):
        for i, piece in enumerate(pieces):
            at = pl.ds(first + (half * count + i) * n, n)
            copies.append(pltpu.make_async_copy(piece.at[half], out.at[at, :], sem.at[i, half]))
            copies[-1].start()
    sums[...] = sum(
        jnp.sum(piece[half].astype(F32), axis=0, keepdims=True)
        for piece in pieces
        for half in range(halves)
    )
    for copy in copies:
        copy.wait()


def stack(pieces, onto=None):
    halves, n, width = pieces[0].shape
    count = len(pieces)
    rows = count * halves * n
    before = [] if onto is None else [onto]
    return pl.pallas_call(
        functools.partial(place_kernel, rows * len(before), count),
        out_shape=[
            jax.ShapeDtypeStruct((2 * rows, width), BF16),
            jax.ShapeDtypeStruct((1, width), F32),
        ],
        in_specs=[ANY] * len(before) + [VMEM] * count,
        out_specs=[ANY, VMEM],
        scratch_shapes=[pltpu.SemaphoreType.DMA((count, halves))],
        input_output_aliases={0: 0} if before else {},
        compiler_params=PARAMS,
        cost_estimate=pl.CostEstimate(
            flops=rows * width, bytes_accessed=4 * rows * width, transcendentals=0
        ),
    )(*before, *pieces)


def turn_kernel(*refs):
    *arrays, out = refs
    n, depth = arrays[0].shape
    tile = 256
    for i, ref in enumerate(arrays):
        for j in range(depth // tile):
            turned = ref[:, j * tile : (j + 1) * tile].T
            out[j * tile : (j + 1) * tile, i * n : (i + 1) * n] = turned if i < 2 else -turned


def turn(arrays):
    n, depth = arrays[0].shape
    return pl.pallas_call(
        turn_kernel,
        out_shape=jax.ShapeDtypeStruct((depth, len(arrays) * n), BF16),
        in_specs=[VMEM] * len(arrays),
        out_specs=VMEM,
        compiler_params=pltpu.CompilerParams(vmem_limit_bytes=16 << 20),
        cost_estimate=pl.CostEstimate(
            flops=0, bytes_accessed=4 * len(arrays) * n * depth, transcendentals=0
        ),
    )(*arrays)


def after(array, *others):
    return lax.optimization_barrier((array, *others))[0]


def together(*groups):
    return lax.optimization_barrier(groups)


def on_device(visible_data, hidden_uniform, visible_uniform, weights, visible_bias, hidden_bias):
    row, col = lax.axis_index("row"), lax.axis_index("col")
    core = col & 1
    block = visible_data.shape[0]
    hiddens = weights.shape[1]
    half = block // 2
    total = block * 16
    q = (row ^ col).astype(jnp.int32).reshape(1)

    def halve(array):
        return (
            lax.dynamic_slice_in_dim(array, core * half, half, 0),
            lax.dynamic_slice_in_dim(array, (1 - core) * half, half, 0),
        )

    def swap(array):
        return flip(array, "col", 1)

    def whole_block(mine, others):
        first = jnp.where(core == 0, mine, others)
        return jnp.concatenate([first, jnp.where(core == 0, others, mine)], axis=0)

    def exchange(sent, axis, step):
        return [flip(a, axis, s * step) for s, a in zip((1, 3, 2), sent)]

    def total_of(own, arrived):
        return own.astype(F32) + sum(a.astype(F32) for a in arrived)

    def quarters(array):
        n = array.shape[0] // 4
        return [array[i * n : (i + 1) * n] for i in range(4)]

    def doubled(array, distance):
        return jnp.concatenate([array, flip(array, "row", distance)], axis=1)

    def sum_zh(partial):
        parts = quarters(partial)
        return total_of(parts[0], exchange([p.astype(BF16) for p in parts[1:]], "row", 4))

    def from_zl_y(own):
        return spread(own, "col", 2) + spread(flip(own, "col", 8), "col", 2)

    def from_zh(pair):
        return jnp.concatenate(spread(pair, "row", 4), axis=1)

    mine, others = halve(visible_data)
    arrived = swap(others)
    visible = jnp.concatenate([mine, arrived], axis=0)
    weights_other = swap(after(weights, arrived))
    visible_lhs, own, sent = forward(q, from_zl_y(visible), weights, weights_other)

    sent, visible_own, hidden_uniform, visible_uniform, bias = together(
        sent, visible_lhs, hidden_uniform, visible_uniform, hidden_bias
    )
    arrived = exchange(sent, "row", 1)
    visible_other = swap(visible_own)
    mine_h, others_h = halve(jnp.log(hidden_uniform) - jnp.log1p(-hidden_uniform))
    mine_v, others_v = halve(jnp.log(visible_uniform) - jnp.log1p(-visible_uniform))
    others = swap(
        jnp.concatenate(
            [others_h, *jnp.split(others_v, 2, axis=1), jnp.broadcast_to(bias, (8, hiddens))], axis=0
        )
    )
    noise_h = jnp.concatenate([mine_h, others[:half]], axis=1)
    others_v = jnp.concatenate([others[half : 2 * half], others[2 * half : 3 * half]], axis=1)
    noise_v = jnp.concatenate([mine_v, others_v], axis=0)
    bias_h = jnp.concatenate([hidden_bias, others[3 * half]])
    arrived, visible_other, noise_h, noise_v, bias_h = together(
        arrived, visible_other, noise_h, noise_v, bias_h
    )
    field_pos = sum_zh(total_of(own, arrived)) + bias_h
    probs_pos = jax.nn.sigmoid(field_pos).astype(BF16)
    sample = jax.nn.sigmoid(2.0 * (field_pos + noise_h)).astype(BF16)

    gathered = jnp.concatenate(spread(sample, "row", 4), axis=0)
    gathered, probs_pos, sample = together(gathered, probs_pos, sample)
    pieces = spread(gathered, "row", 1)
    others = swap(jnp.concatenate([probs_pos[:, hiddens:], sample[:, hiddens:]], axis=0))
    pos = jnp.stack([probs_pos[:, :hiddens], others[:half]])
    hidden_sample = whole_block(sample[:, :hiddens], others[half:])
    pos = doubled(pos, 4)
    pieces, pos = together(pieces, pos)
    own0, own1, sent0, sent1 = backward(q, pieces, weights, weights_other)

    sent0, sent1, pos = together(sent0, sent1, pos)
    arrived1 = exchange(sent1, "col", 2)
    arrived0 = exchange(sent0, "col", 2)
    pos = doubled(pos, 12)
    partial = total_of(own1, arrived1).astype(BF16)
    field_neg = total_of(own0, arrived0) + flip(partial, "col", 8).astype(F32) + visible_bias
    recon = jax.nn.sigmoid(2.0 * (field_neg + noise_v)).astype(BF16)

    recon, pos = together(recon, pos)
    pieces = from_zl_y(recon)
    pos = doubled(pos, 1)
    pieces, pos = together(pieces, pos)
    recon_lhs, own, sent = forward(q, pieces, weights, weights_other)

    sent, recon_own = together(sent, recon_lhs)
    arrived = exchange(sent, "row", 1)
    recon_other = swap(recon_own)
    partial = total_of(own, arrived)
    partial, recon_other, pos = together(partial, recon_other, pos)
    pos = [pos, flip(pos, "row", 3)]
    field_back = sum_zh(partial) + bias_h
    probs_neg = jax.nn.sigmoid(field_back).astype(BF16)

    pair = from_zh(jnp.stack([probs_neg[:, :hiddens], swap(probs_neg[:, hiddens:])]))
    pair, pos, visible_own, visible_other, recon_own, recon_other, recon = together(
        pair, pos, visible_own, visible_other, recon_own, recon_other, recon
    )
    neg = spread(pair, "row", 1)
    right, sum_pos = stack(pos)
    turned = turn([visible_own, visible_other, recon_own, recon_other])
    grad_visible = (
        jnp.sum(visible_own.astype(F32) + visible_other.astype(F32), axis=0)
        - jnp.sum(recon_own.astype(F32) + recon_other.astype(F32), axis=0)
    ) / total
    place = row_to_index(row ^ col) * half
    reconstruction = whole_block(
        recon[:half], lax.dynamic_slice_in_dim(recon_other, place, half, 0)
    )
    neg, turned, right, sum_pos, grad_visible, reconstruction = together(
        neg, turned, right, sum_pos, grad_visible, reconstruction
    )
    right, sum_neg = stack(neg, right)
    grad_hidden = (sum_pos - sum_neg) / total
    grad_weights = (jnp.dot(turned, right, preferred_element_type=F32) / total).astype(BF16)
    return (grad_weights, grad_visible, grad_hidden.reshape(-1), hidden_sample, reconstruction)


def solution(mesh):
    placed = (
        P("col", "row"),
        P("row", "col"),
        P("col", "row"),
        P("row", "col"),
        P("row"),
        P("col"),
    )
    return jax.shard_map(
        on_device,
        mesh=mesh,
        in_specs=placed,
        out_specs=(P("row", "col"), P("row"), P("col"), P("row", "col"), P("col", "row")),
        check_vma=False,
    )
```
